1024 devices in a mesh: blk: 16 (over z_lo, y), grp: 64 (over x, z_hi, core).
Axes of the slice: x: 8, y: 8, z: 8 (z_hi: 4, z_lo: 2; z = z_hi * 2 + z_lo), core: 2. Of those that a mesh axis runs over, the one named last changes fastest.
Arguments:
- queries: bfloat16 [32, 128, 1280], P('blk'), may hold values from -8 to 8
- query_lengths: int32 [32], P('blk'), may hold values from 32 to 128, as said below
- targets: bfloat16 [4096, 128, 1280], P(('blk', 'grp')), may hold values from -8 to 8
- target_lengths: int32 [4096], P(('blk', 'grp')), may hold values from 32 to 128, as said below
Outputs:
- profile: float32 [32, 128, 1280], P('blk', 'grp')
- similarity: float32 [32, 1024], P('blk', 'grp')
The draws below stay inside these ranges and needn't reach their ends.
Inputs may be any that keep to these rules, and one draw needn't show every extreme that they name: The first query_lengths[q] residues of query q are valid, the rest is padding; some query has all 128. The first target_lengths[t] residues of target t are valid, the rest is padding; some target has all 128.
All inputs are finite; a program needn't handle non-finite values.
Results may differ from the reference program's by a relative error of at most 0.00079.
Values may be sent and summed in bfloat16 or wider, within the bound.
No kernel may reach another device: no remote copies, remote signals or barrier semaphores. Data moves between devices by JAX's collectives and lax.ppermute only.
A program may use at most 32 MiB of HBM per device.

```python
import math
import jax
import jax.numpy as jnp
from jax import lax

D = 1280
L = 128
QDEV = 2
TB = 4
STEPS = 3
NQ = 32
NT = 4096
N_BLK = 16
N_GRP = 64


def base_values(key, shape):
    return jnp.clip(jax.random.normal(key, shape, jnp.float32), -6.0, 6.0)


def draw_queries(key, part):
    values = base_values(jax.random.fold_in(key, 1), (NQ, L, D))
    return jnp.clip(values, -8.0, 8.0).astype(jnp.bfloat16)


def draw_targets(key, part):
    values = base_values(jax.random.fold_in(key, 3), (NT, L, D))
    return jnp.clip(values, -8.0, 8.0).astype(jnp.bfloat16)


def draw_query_lengths(key, part):
    drawn = jax.random.randint(jax.random.fold_in(key, 11), (NQ,), L // 4, L + 1, jnp.int32)
    chosen = jax.random.randint(jax.random.fold_in(key, 12), (), 0, NQ, jnp.int32)
    return drawn.at[chosen].set(L)


def draw_target_lengths(key, part):
    drawn = jax.random.randint(jax.random.fold_in(key, 13), (NT,), L // 4, L + 1, jnp.int32)
    chosen = jax.random.randint(jax.random.fold_in(key, 14), (), 0, NT, jnp.int32)
    return drawn.at[chosen].set(L)


def setup_inputs(seed: int = 0) -> dict:
    splits = jax.random.split(jax.random.key(seed), 5)
    return {
        "queries": draw_queries(jax.random.fold_in(splits[4], 71), 0),
        "query_lengths": draw_query_lengths(jax.random.fold_in(splits[4], 71), 0),
        "targets": draw_targets(jax.random.fold_in(splits[4], 71), 0),
        "target_lengths": draw_target_lengths(jax.random.fold_in(splits[4], 71), 0),
    }


def align_pair(query_rows, query_len, target_rows, target_len):
    scale = 3.0 / math.sqrt(query_rows.shape[-1])
    scores = jnp.einsum('qid,mjd->qmij', query_rows.astype(jnp.float32), target_rows.astype(jnp.float32)) * scale
    positions = jnp.arange(query_rows.shape[1], dtype=jnp.int32)
    row_ok = positions[None, :] < query_len[:, None]
    col_ok = positions[None, :] < target_len[:, None]
    row_mask = row_ok[:, None, :, None]
    col_mask = col_ok[None, :, None, :]
    row_top = lax.optimization_barrier(jnp.max(jnp.where(col_mask, scores, -jnp.inf), axis=3, keepdims=True))
    row_exp = jnp.where(col_mask, jnp.exp(scores - row_top), 0.0)
    row_soft = jnp.where(row_mask, row_exp / lax.optimization_barrier(jnp.sum(row_exp, axis=3, keepdims=True)), 0.0)
    col_top = lax.optimization_barrier(jnp.max(jnp.where(row_mask, scores, -jnp.inf), axis=2, keepdims=True))
    col_exp = jnp.where(row_mask, jnp.exp(scores - col_top), 0.0)
    col_soft = jnp.where(col_mask, col_exp / lax.optimization_barrier(jnp.sum(col_exp, axis=2, keepdims=True)), 0.0)
    weights = row_soft + col_soft - row_soft * col_soft
    similarity = lax.optimization_barrier(jnp.sum(weights * scores, axis=(2, 3))) / lax.optimization_barrier(jnp.sum(weights, axis=(2, 3)))
    rounded = lax.optimization_barrier(row_soft.astype(jnp.bfloat16))
    profile = jnp.einsum('qmij,mjd->qid', rounded.astype(jnp.float32), target_rows.astype(jnp.float32))
    return (similarity, profile)

def reference(queries, query_lengths, targets, target_lengths):
    query_sets = queries.reshape(N_BLK, QDEV, L, D)
    query_lens = query_lengths.reshape(N_BLK, QDEV)
    target_sets = targets.reshape(N_BLK, N_GRP * TB, L, D)
    target_lens = target_lengths.reshape(N_BLK, N_GRP * TB)
    profile_scale = 1.0 / math.sqrt(N_GRP * TB * (STEPS + 1))

    def one_set(inputs):
        cycle_index, query_rows, query_len = inputs
        running = jnp.zeros((QDEV, L, D), jnp.float32)
        gathered = []
        for offset in range(STEPS + 1):
            source = ((cycle_index - offset) % N_BLK).astype(jnp.int32)
            target_rows = lax.dynamic_index_in_dim(target_sets, source, 0, keepdims=False)
            target_len = lax.dynamic_index_in_dim(target_lens, source, 0, keepdims=False)
            pair_sim, pair_prof = align_pair(query_rows, query_len, target_rows, target_len)
            running = running + pair_prof
            gathered.append(pair_sim.reshape(QDEV, N_GRP, TB))
        similarity = jnp.stack(gathered, axis=2).reshape(QDEV, N_GRP * (STEPS + 1) * TB)
        return (running * profile_scale, similarity)
    profile, similarity = lax.map(one_set, (jnp.arange(N_BLK, dtype=jnp.int32), query_sets, query_lens))
    return (profile.reshape(NQ, L, D), similarity.reshape(NQ, N_GRP * (STEPS + 1) * TB))
```

```python
import math

import jax
import jax.numpy as jnp
from jax import lax
from jax.experimental import pallas as pl
from jax.experimental.pallas import tpu as pltpu
from jax.sharding import Mesh
from jax.sharding import PartitionSpec as P

BLK = ("zl", "y")
GRP = ("x", "zh", "core")
STEPS = 3
NX, NZ = 8, 4
F32 = jnp.float32
BF16 = jnp.bfloat16


def soft_block(q_ref, t_ref, qlen_ref, tlen_ref, offset, sims):
    queries, length, width = q_ref.shape
    blocks = t_ref.shape[0]
    scale = 3.0 / math.sqrt(width)
    scores = (
        lax.dot_general(
            q_ref[...].reshape(queries * length, width),
            t_ref[...].reshape(blocks * length, width),
            (((1,), (1,)), ((), ())),
            preferred_element_type=F32,
        )
        * scale
    )
    lanes = lax.broadcasted_iota(jnp.int32, (length, length), 1)
    rows = lax.broadcasted_iota(jnp.int32, (length, length), 0)
    place_row = lax.broadcasted_iota(jnp.int32, sims.shape, 0)
    place_lane = lax.broadcasted_iota(jnp.int32, sims.shape, 1)
    stacked = []
    for q in range(queries):
        row_ok = rows < qlen_ref[q]
        row_on = lax.broadcasted_iota(jnp.int32, (length, 1), 0) < qlen_ref[q]
        pieces = []
        for m in range(blocks):
            col_ok = lanes < tlen_ref[m]
            col_on = lax.broadcasted_iota(jnp.int32, (1, length), 1) < tlen_ref[m]
            s = scores[q * length : (q + 1) * length, m * length : (m + 1) * length]
            by_row = jnp.where(col_ok, s, -jnp.inf)
            row_exp = jnp.exp(by_row - jnp.max(by_row, axis=1, keepdims=True))
            row_soft = row_exp * jnp.where(row_on, 1.0 / jnp.sum(row_exp, axis=1, keepdims=True), 0.0)
            by_col = jnp.where(row_ok, s, -jnp.inf)
            col_exp = jnp.exp(by_col - jnp.max(by_col, axis=0, keepdims=True))
            col_soft = col_exp * jnp.where(col_on, 1.0 / jnp.sum(col_exp, axis=0, keepdims=True), 0.0)
            weights = row_soft + col_soft - row_soft * col_soft
            over = jnp.sum(jnp.sum(weights * s, axis=0, keepdims=True), axis=1, keepdims=True)
            under = jnp.sum(jnp.sum(weights, axis=0, keepdims=True), axis=1, keepdims=True)
            here = jnp.logical_and(place_row == q, place_lane == offset * blocks + m)
            sims = jnp.where(here, over / under, sims)
            pieces.append(row_soft.astype(BF16))
        stacked.append(jnp.concatenate(pieces, axis=1))
    return jnp.concatenate(stacked, axis=0), sims


def ordered(align, core_ref):
    total = align.shape[0]
    p = lax.broadcasted_iota(jnp.int32, (total, total), 0)
    i = lax.broadcasted_iota(jnp.int32, (total, total), 1)
    core = jnp.bitwise_xor(p >> 8, core_ref[0])
    source = ((p >> 1) & 3) * 128 + ((p >> 3) & 31) * 4 + core * 2 + (p & 1)
    pick = jnp.where(i == source, 1.0, 0.0).astype(BF16)
    return jnp.dot(pick, align, preferred_element_type=F32).astype(BF16)


def own_kernel(qlen_ref, tlen_ref, q_ref, t_ref, align_ref, sims_ref):
    align, sims = soft_block(q_ref, t_ref, qlen_ref, tlen_ref, 0, jnp.zeros(sims_ref.shape, F32))
    align_ref[...] = align
    sims_ref[...] = sims


def rest_kernel(
    core_ref, qlen_ref, qlen2_ref, tlen_ref, tlen1_ref, q_ref, q2_ref, t_ref, t1_ref, align_ref, sims_ref,
    mine_ref, theirs_ref, sims01_ref, sims23_ref, every_ref,
):
    flat = (t_ref.shape[0] * t_ref.shape[1], t_ref.shape[2])
    rows, columns = align_ref.shape
    every_ref[:rows, :columns] = align_ref[...]
    every_ref[rows:, :columns], sims = soft_block(q2_ref, t_ref, qlen2_ref, tlen_ref, 2, jnp.zeros(sims_ref.shape, F32))
    every_ref[:rows, columns:], sims01_ref[...] = soft_block(q_ref, t1_ref, qlen_ref, tlen1_ref, 1, sims_ref[...])
    every_ref[rows:, columns:], sims23_ref[...] = soft_block(q2_ref, t1_ref, qlen2_ref, tlen1_ref, 3, sims)
    align = ordered(every_ref[...], core_ref)
    partial = jnp.dot(align[:, :columns], t_ref[...].reshape(flat), preferred_element_type=F32)
    partial += jnp.dot(align[:, columns:], t1_ref[...].reshape(flat), preferred_element_type=F32)
    mine_ref[...] = partial[:rows].reshape(mine_ref.shape)
    theirs_ref[...] = partial[rows:].reshape(theirs_ref.shape)


def pack_kernel(mine_ref, theirs_ref, packed_ref, total_ref):
    total_ref[...] = mine_ref[...] + theirs_ref[...]
    top = jnp.max(jnp.abs(total_ref[...]), axis=0)
    top = jnp.max(jnp.max(top, axis=0, keepdims=True), axis=1, keepdims=True)
    power = jnp.floor(14.5 - jnp.log(jnp.maximum(top, 1e-30)) * (1.0 / math.log(2.0)))
    width = mine_ref.shape[2]
    packed_ref[:, :, :width] = total_ref[...] * jnp.exp2(power)[None]
    side = (mine_ref.shape[0], mine_ref.shape[1], packed_ref.shape[2] - width)
    packed_ref[:, :, width:] = jnp.broadcast_to(power[None], side)


def unpacked_sum(packed_ref, width):
    total = jnp.zeros((packed_ref.shape[1], width), F32)
    for n in range(packed_ref.shape[0]):
        total += packed_ref[n, :, :width] * jnp.exp2(-packed_ref[n, :, width : width + 1])
    return total


def hand_on(total, sims_ref, own_ref, message_ref):
    half = own_ref.shape[0]
    own_ref[...] = total[:half]
    message_ref[...] = jnp.zeros(message_ref.shape, F32)
    message_ref[0:half, :] = total[half:]
    message_ref[half : half + 2, 0 : sims_ref.shape[1]] = sims_ref[0:2, :]


def sum_kernel(packed_ref, total_ref):
    total_ref[...] = unpacked_sum(packed_ref, total_ref.shape[1])


def tail_kernel(pieces_ref, sims_ref, own_ref, message_ref):
    hand_on(jnp.sum(pieces_ref[...], axis=0), sims_ref, own_ref, message_ref)


def packed_tail_kernel(packed_ref, sims_ref, own_ref, message_ref):
    hand_on(unpacked_sum(packed_ref, own_ref.shape[1]), sims_ref, own_ref, message_ref)


SMEM = pl.BlockSpec(memory_space=pltpu.SMEM)
VMEM = pl.BlockSpec(memory_space=pltpu.VMEM)


def call(kernel, scalars, arrays, outs, flops, name, scratch=()):
    moved = sum(a.size * a.dtype.itemsize for a in [*arrays, *outs])
    return pl.pallas_call(
        kernel,
        out_shape=outs,
        in_specs=[SMEM] * len(scalars) + [VMEM] * len(arrays),
        out_specs=[VMEM] * len(outs),
        scratch_shapes=list(scratch),
        cost_estimate=pl.CostEstimate(flops=flops, bytes_accessed=moved, transcendentals=0),
        compiler_params=pltpu.CompilerParams(vmem_limit_bytes=20 << 20),
        name=name,
    )(*scalars, *arrays)


def moved_by(array, by):
    length = lax.axis_size(BLK)
    return lax.ppermute(array, BLK, [(i, (i + by) % length) for i in range(length)])


def shards(queries, query_lengths, targets, target_lengths):
    count, length, width = queries.shape
    blocks = targets.shape[0]
    profile_scale = 1.0 / math.sqrt(lax.axis_size(GRP) * blocks * (STEPS + 1))
    core = lax.axis_index("core").reshape(1)
    struct = jax.ShapeDtypeStruct
    pair_flops = 2 * count * blocks * length * length * width

    targets1 = moved_by(targets, 1)
    queries2 = moved_by(queries, -2)
    lengths1 = moved_by(target_lengths, 1)
    query_lengths2 = moved_by(query_lengths, -2)

    sims_shape = struct((8, 128), F32)
    rows = count * length
    align, sims = call(
        own_kernel, [query_lengths, target_lengths], [queries, targets],
        [struct((rows, blocks * length), BF16), sims_shape], pair_flops, "own_pairs",
    )
    owned = rows // (NX * NZ)
    halves = struct((NX * NZ, owned, width), F32)
    mine, theirs, sims01, sims23 = call(
        rest_kernel, [core, query_lengths, query_lengths2, target_lengths, lengths1],
        [queries, queries2, targets, targets1, align, sims],
        [halves, halves, sims_shape, sims_shape], 8 * pair_flops, "other_pairs",
        [pltpu.VMEM((2 * rows, 2 * blocks * length), BF16)],
    )

    theirs = lax.ppermute(theirs, "core", [(0, 1), (1, 0)])
    packed_shape = struct((NX * NZ, owned, width + 128), F32)
    (packed,) = call(
        pack_kernel, [], [mine, theirs], [packed_shape], 8 * mine.size, "pack", [pltpu.VMEM(mine.shape, F32)]
    )
    half = owned // 2
    ends = [struct((half, width), F32), struct((owned, width), F32)]
    packed = lax.all_to_all(packed.astype(jnp.float16), ("x", "zh"), 0, 0, tiled=True).astype(F32)
    own, message = call(packed_tail_kernel, [], [packed, sims23], ends, packed.size, "tail")
    message = moved_by(message, 2)
    profile = (own + message[:half]) * profile_scale
    columns = blocks * (STEPS + 1)
    similarity = sims01[:count, :columns] + message[half : half + count, :columns]
    return (profile.reshape(count, half // count, width), similarity)


def solution(mesh):
    cut = Mesh(mesh.devices.reshape(2, 8, NX, NZ, 2), BLK + GRP)
    in_specs = (P(BLK, None, None), P(BLK), P(BLK + GRP, None, None), P(BLK + GRP))
    out_specs = (P(BLK, GRP, None), P(BLK, GRP))
    return jax.shard_map(shards, mesh=cut, in_specs=in_specs, out_specs=out_specs, check_vma=False)
```

```python
import functools
import math

import jax
import jax.numpy as jnp
from jax import lax
from jax.experimental import pallas as pl
from jax.experimental.pallas import tpu as pltpu
from jax.sharding import Mesh
from jax.sharding import PartitionSpec as P

BLK = ("zl", "y")
GRP = ("x", "zh", "core")
STEPS = 3
MARK = 256.0
NX, NZ = 8, 4
F32 = jnp.float32
BF16 = jnp.bfloat16


def soft_block(q_ref, t_ref, qlen_ref, tlen_ref, lane, sims, first=0):
    queries, length, width = q_ref.shape
    blocks = t_ref.shape[0]
    scale = 3.0 / math.sqrt(width)
    scores = (
        lax.dot_general(
            q_ref[...].reshape(queries * length, width),
            t_ref[...].reshape(blocks * length, width),
            (((1,), (1,)), ((), ())),
            preferred_element_type=F32,
        )
        * scale
    )
    lanes = lax.broadcasted_iota(jnp.int32, (length, length), 1)
    place_row = lax.broadcasted_iota(jnp.int32, sims.shape, 0)
    place_lane = lax.broadcasted_iota(jnp.int32, sims.shape, 1)
    stacked = []
    for q in range(queries):
        if qlen_ref is None:
            row_on = q_ref[q, :, 0:128].astype(F32)[:, 0:1] < 0.5 * MARK
        else:
            row_on = lax.broadcasted_iota(jnp.int32, (length, 1), 0) < qlen_ref[q]
        row_ok = jnp.broadcast_to(row_on, (length, length))
        pieces = []
        for m in range(blocks):
            col_ok = lanes < tlen_ref[first + m]
            col_on = lax.broadcasted_iota(jnp.int32, (1, length), 1) < tlen_ref[first + m]
            s = scores[q * length : (q + 1) * length, m * length : (m + 1) * length]
            by_row = jnp.where(col_ok, s, -jnp.inf)
            row_exp = jnp.exp(by_row - jnp.max(by_row, axis=1, keepdims=True))
            row_soft = row_exp * jnp.where(row_on, 1.0 / jnp.sum(row_exp, axis=1, keepdims=True), 0.0)
            by_col = jnp.where(row_ok, s, -jnp.inf)
            col_exp = jnp.exp(by_col - jnp.max(by_col, axis=0, keepdims=True))
            col_soft = col_exp * jnp.where(col_on, 1.0 / jnp.sum(col_exp, axis=0, keepdims=True), 0.0)
            weights = row_soft + col_soft - row_soft * col_soft
            over = jnp.sum(jnp.sum(weights * s, axis=0, keepdims=True), axis=1, keepdims=True)
            under = jnp.sum(jnp.sum(weights, axis=0, keepdims=True), axis=1, keepdims=True)
            here = jnp.logical_and(place_row == q, place_lane == lane + m)
            sims = jnp.where(here, over / under, sims)
            pieces.append(row_soft.astype(BF16))
        stacked.append(jnp.concatenate(pieces, axis=1))
    return jnp.concatenate(stacked, axis=0), sims


def owner_order(core_ref, total, rows):
    p = lax.broadcasted_iota(jnp.int32, (total, rows), 0)
    i = lax.broadcasted_iota(jnp.int32, (total, rows), 1)
    core = jnp.bitwise_xor(p >> 8, core_ref[0])
    source = ((p >> 1) & 3) * 128 + ((p >> 3) & 31) * 4 + core * 2 + (p & 1)
    return jnp.where(i == source, 1.0, 0.0).astype(BF16)


def share(core_ref, first, second, t_ref):
    align = jnp.concatenate([first, second], axis=0)
    pick = owner_order(core_ref, align.shape[0], align.shape[0])
    align = jnp.dot(pick, align, preferred_element_type=F32).astype(BF16)
    block = t_ref[...].reshape(t_ref.shape[0] * t_ref.shape[1], t_ref.shape[2])
    return jnp.dot(align, block, preferred_element_type=F32)


def own_kernel(qlen_ref, tlen_ref, q_ref, t_ref, align_ref, sims_ref):
    align, sims = soft_block(q_ref, t_ref, qlen_ref, tlen_ref, 0, jnp.zeros(sims_ref.shape, F32))
    align_ref[...] = align
    sims_ref[...] = sims


def near_kernel(core_ref, tlen_ref, q2_ref, t_ref, align_ref, partial_ref, sims23_ref):
    second, sims = soft_block(q2_ref, t_ref, None, tlen_ref, 8, jnp.zeros(sims23_ref.shape, F32))
    partial_ref[...] = share(core_ref, align_ref[...], second, t_ref)
    sims23_ref[...] = sims


def far_step(first, core_ref, qlen_ref, tlen1_ref, q_ref, q2_ref, t1_ref, partial_ref, sims01_ref, sims23_ref):
    align, sims01 = soft_block(q_ref, t1_ref, qlen_ref, tlen1_ref, 4 + first, sims01_ref[...], first)
    second, sims23 = soft_block(q2_ref, t1_ref, None, tlen1_ref, 12 + first, sims23_ref[...], first)
    return partial_ref[...] + share(core_ref, align, second, t1_ref), sims01, sims23


def middle_kernel(*refs):
    *ins, out_ref, out01_ref, out23_ref = refs
    out_ref[...], out01_ref[...], out23_ref[...] = far_step(0, *ins)


def last_kernel(first, *refs):
    *ins, mine_ref, theirs_ref, out01_ref, out23_ref = refs
    partial, out01_ref[...], out23_ref[...] = far_step(first, *ins)
    half = partial.shape[0] // 2
    mine_ref[...] = partial[:half].reshape(mine_ref.shape)
    theirs_ref[...] = partial[half:].reshape(theirs_ref.shape)


def final_kernel(scale, own_ref, message_ref, sims_ref, profile_ref, similarity_ref):
    count, rows = profile_ref.shape[:2]
    columns = similarity_ref.shape[1]
    total = (own_ref[...] + message_ref[0 : count * rows, :]) * scale
    for q in range(count):
        profile_ref[q] = total[q * rows : (q + 1) * rows]
    similarity_ref[...] = sims_ref[0:count, 0:columns] + message_ref[count * rows : count * rows + count, 0:columns]


def pack_kernel(mine_ref, theirs_ref, packed_ref, total_ref):
    total_ref[...] = mine_ref[...] + theirs_ref[...]
    top = jnp.max(jnp.abs(total_ref[...]), axis=0)
    top = jnp.max(jnp.max(top, axis=0, keepdims=True), axis=1, keepdims=True)
    power = jnp.floor(14.5 - jnp.log(jnp.maximum(top, 1e-30)) * (1.0 / math.log(2.0)))
    width = mine_ref.shape[2]
    packed_ref[:, :, :width] = total_ref[...] * jnp.exp2(power)[None]
    side = (mine_ref.shape[0], mine_ref.shape[1], packed_ref.shape[2] - width)
    packed_ref[:, :, width:] = jnp.broadcast_to(power[None], side)


def unpacked_sum(packed_ref, width):
    total = jnp.zeros((packed_ref.shape[1], width), F32)
    for n in range(packed_ref.shape[0]):
        total += packed_ref[n, :, :width] * jnp.exp2(-packed_ref[n, :, width : width + 1])
    return total


def hand_on(total, sims_ref, own_ref, message_ref):
    half = own_ref.shape[0]
    own_ref[...] = total[:half]
    message_ref[...] = jnp.zeros(message_ref.shape, F32)
    message_ref[0:half, :] = total[half:]
    message_ref[half : half + 2, 0 : sims_ref.shape[1]] = sims_ref[0:2, :]


def sum_kernel(packed_ref, total_ref):
    total_ref[...] = unpacked_sum(packed_ref, total_ref.shape[1])


def tail_kernel(pieces_ref, sims_ref, own_ref, message_ref):
    hand_on(jnp.sum(pieces_ref[...], axis=0), sims_ref, own_ref, message_ref)


def packed_tail_kernel(packed_ref, sims_ref, own_ref, message_ref):
    hand_on(unpacked_sum(packed_ref, own_ref.shape[1]), sims_ref, own_ref, message_ref)


SMEM = pl.BlockSpec(memory_space=pltpu.SMEM)
VMEM = pl.BlockSpec(memory_space=pltpu.VMEM)


def call(kernel, scalars, arrays, outs, flops, name, scratch=()):
    moved = sum(a.size * a.dtype.itemsize for a in [*arrays, *outs])
    return pl.pallas_call(
        kernel,
        out_shape=outs,
        in_specs=[SMEM] * len(scalars) + [VMEM] * len(arrays),
        out_specs=[VMEM] * len(outs),
        scratch_shapes=list(scratch),
        cost_estimate=pl.CostEstimate(flops=flops, bytes_accessed=moved, transcendentals=0),
        compiler_params=pltpu.CompilerParams(vmem_limit_bytes=20 << 20),
        name=name,
    )(*scalars, *arrays)


def moved_by(array, by):
    length = lax.axis_size(BLK)
    return lax.ppermute(array, BLK, [(i, (i + by) % length) for i in range(length)])


def shards(queries, query_lengths, targets, target_lengths):
    count, length, width = queries.shape
    blocks = targets.shape[0]
    profile_scale = 1.0 / math.sqrt(lax.axis_size(GRP) * blocks * (STEPS + 1))
    core = lax.axis_index("core").reshape(1)
    struct = jax.ShapeDtypeStruct
    pair_flops = 2 * count * blocks * length * length * width

    targets1 = [moved_by(targets, 1)]
    spot = lax.broadcasted_iota(jnp.int32, (1, length, width), 1) >= query_lengths[core[0]]
    spot = jnp.logical_and(spot, lax.broadcasted_iota(jnp.int32, (1, length, width), 2) == 0)
    mine2 = jnp.where(spot, jnp.asarray(MARK, BF16), lax.dynamic_slice_in_dim(queries, core[0], 1))
    mine2 = moved_by(mine2, -2)
    lengths1 = moved_by(target_lengths, 1)

    sims_shape = struct((8, 128), F32)
    rows = count * length
    align, sims01 = call(
        own_kernel, [query_lengths, target_lengths], [queries, targets],
        [struct((rows, blocks * length), BF16), sims_shape], pair_flops, "own_pairs",
    )
    mine2, align = lax.optimization_barrier((mine2, align))
    other2 = lax.ppermute(mine2, "core", [(0, 1), (1, 0)])
    queries2 = jnp.where(core[0] == 0, jnp.concatenate([mine2, other2]), jnp.concatenate([other2, mine2]))
    partial_shape = struct((2 * rows, width), F32)
    partial, sims23 = call(
        near_kernel, [core, target_lengths], [queries2, targets, align],
        [partial_shape, sims_shape], 3 * pair_flops, "near_pairs",
    )
    scalars = [core, query_lengths, lengths1]
    owned = rows // (NX * NZ)
    halves = struct((NX * NZ, owned, width), F32)
    mine, theirs, sims01, sims23 = call(
        functools.partial(last_kernel, 0), scalars, [queries, queries2, targets1[-1], partial, sims01, sims23],
        [halves, halves, sims_shape, sims_shape], 4 * pair_flops, "last_pairs",
    )

    theirs = lax.ppermute(theirs, "core", [(0, 1), (1, 0)])
    packed_shape = struct((NX * NZ, owned, width + 128), F32)
    (packed,) = call(
        pack_kernel, [], [mine, theirs], [packed_shape], 8 * mine.size, "pack", [pltpu.VMEM(mine.shape, F32)]
    )
    half = owned // 2
    ends = [struct((half, width), F32), struct((owned, width), F32)]
    packed = lax.all_to_all(packed.astype(jnp.float16), ("x", "zh"), 0, 0, tiled=True).astype(F32)
    own, message = call(packed_tail_kernel, [], [packed, sims23], ends, packed.size, "tail")
    message = moved_by(message, 2)
    profile, similarity = call(
        functools.partial(final_kernel, profile_scale), [], [own, message, sims01],
        [struct((count, half // count, width), F32), struct((count, blocks * (STEPS + 1)), F32)], own.size, "final",
    )
    return (profile, similarity)


def solution(mesh):
    cut = Mesh(mesh.devices.reshape(2, 8, NX, NZ, 2), BLK + GRP)
    in_specs = (P(BLK, None, None), P(BLK), P(BLK + GRP, None, None), P(BLK + GRP))
    out_specs = (P(BLK, GRP, None), P(BLK, GRP))
    return jax.shard_map(shards, mesh=cut, in_specs=in_specs, out_specs=out_specs, check_vma=False)
```

```python
import functools
import math

import jax
import jax.numpy as jnp
from jax import lax
from jax.experimental import pallas as pl
from jax.experimental.pallas import tpu as pltpu
from jax.sharding import Mesh
from jax.sharding import PartitionSpec as P

BLK = ("zl", "y")
GRP = ("x", "zh", "core")
STEPS = 3
MARK = 256.0
NX, NZ = 8, 4
F32 = jnp.float32
BF16 = jnp.bfloat16


def soft_block(q_ref, t_ref, qlen_ref, tlen_ref, lane, sims):
    queries, length, width = q_ref.shape
    blocks = t_ref.shape[0]
    scale = 3.0 / math.sqrt(width)
    scores = (
        lax.dot_general(
            q_ref[...].reshape(queries * length, width),
            t_ref[...].reshape(blocks * length, width),
            (((1,), (1,)), ((), ())),
            preferred_element_type=F32,
        )
        * scale
    )
    lanes = lax.broadcasted_iota(jnp.int32, (length, length), 1)
    place_row = lax.broadcasted_iota(jnp.int32, sims.shape, 0)
    place_lane = lax.broadcasted_iota(jnp.int32, sims.shape, 1)
    stacked = []
    for q in range(queries):
        if qlen_ref is None:
            row_on = q_ref[q, :, 0:128].astype(F32)[:, 0:1] < 0.5 * MARK
        else:
            row_on = lax.broadcasted_iota(jnp.int32, (length, 1), 0) < qlen_ref[q]
        row_ok = jnp.broadcast_to(row_on, (length, length))
        pieces = []
        for m in range(blocks):
            col_ok = lanes < tlen_ref[m]
            col_on = lax.broadcasted_iota(jnp.int32, (1, length), 1) < tlen_ref[m]
            s = scores[q * length : (q + 1) * length, m * length : (m + 1) * length]
            by_row = jnp.where(col_ok, s, -jnp.inf)
            row_exp = jnp.exp(by_row - jnp.max(by_row, axis=1, keepdims=True))
            row_soft = row_exp * jnp.where(row_on, 1.0 / jnp.sum(row_exp, axis=1, keepdims=True), 0.0)
            by_col = jnp.where(row_ok, s, -jnp.inf)
            col_exp = jnp.exp(by_col - jnp.max(by_col, axis=0, keepdims=True))
            col_soft = col_exp * jnp.where(col_on, 1.0 / jnp.sum(col_exp, axis=0, keepdims=True), 0.0)
            weights = row_soft + col_soft - row_soft * col_soft
            over = jnp.sum(jnp.sum(weights * s, axis=0, keepdims=True), axis=1, keepdims=True)
            under = jnp.sum(jnp.sum(weights, axis=0, keepdims=True), axis=1, keepdims=True)
            here = jnp.logical_and(place_row == q, place_lane == lane + m)
            sims = jnp.where(here, over / under, sims)
            pieces.append(row_soft.astype(BF16))
        stacked.append(jnp.concatenate(pieces, axis=1))
    return jnp.concatenate(stacked, axis=0), sims


def owner_order(core_ref, total, rows):
    p = lax.broadcasted_iota(jnp.int32, (total, rows), 0)
    i = lax.broadcasted_iota(jnp.int32, (total, rows), 1)
    core = jnp.bitwise_xor(p >> 8, core_ref[0])
    source = ((p >> 1) & 3) * 128 + ((p >> 3) & 31) * 4 + core * 2 + (p & 1)
    return jnp.where(i == source, 1.0, 0.0).astype(BF16)


def in_owner_order(core_ref, first, second):
    align = jnp.concatenate([first, second], axis=0)
    pick = owner_order(core_ref, align.shape[0], align.shape[0])
    return jnp.dot(pick, align, preferred_element_type=F32).astype(BF16)


def profile_of(align, t_ref):
    block = t_ref[...].reshape(t_ref.shape[0] * t_ref.shape[1], t_ref.shape[2])
    return jnp.dot(align, block, preferred_element_type=F32)


def fetch_kernel(core_ref, qlen_ref, q_ref, out_ref):
    shape = (out_ref.shape[1], 128)
    padding = lax.broadcasted_iota(jnp.int32, shape, 0) >= qlen_ref[core_ref[0]]
    spot = jnp.logical_and(padding, lax.broadcasted_iota(jnp.int32, shape, 1) == 0)
    out_ref[0] = q_ref[core_ref[0]]
    out_ref[0, :, 0:128] = jnp.where(spot, MARK, q_ref[core_ref[0], :, 0:128].astype(F32)).astype(BF16)


def own_kernel(qlen_ref, tlen_ref, q_ref, t_ref, align_ref, sims_ref):
    align, sims = soft_block(q_ref, t_ref, qlen_ref, tlen_ref, 0, jnp.zeros(sims_ref.shape, F32))
    align_ref[...] = align
    sims_ref[...] = sims


def near_kernel(core_ref, tlen_ref, q2_ref, t_ref, align_ref, mine_ref, theirs_ref, sims23_ref):
    second, sims = soft_block(q2_ref, t_ref, None, tlen_ref, 8, jnp.zeros(sims23_ref.shape, F32))
    partial = profile_of(in_owner_order(core_ref, align_ref[...], second), t_ref)
    half = partial.shape[0] // 2
    mine_ref[...] = partial[:half]
    theirs_ref[...] = partial[half:]
    sims23_ref[...] = sims


def far_kernel(
    core_ref, qlen_ref, tlen1_ref, q_ref, q2_ref, t1_ref, near_ref, sims01_ref, sims23_ref,
    theirs_ref, align_ref, out01_ref, out23_ref,
):
    first, out01_ref[...] = soft_block(q_ref, t1_ref, qlen_ref, tlen1_ref, 4, sims01_ref[...])
    second, out23_ref[...] = soft_block(q2_ref, t1_ref, None, tlen1_ref, 12, sims23_ref[...])
    align = in_owner_order(core_ref, first, second)
    half = align.shape[0] // 2
    theirs_ref[...] = (near_ref[...] + profile_of(align[half:], t1_ref)).reshape(theirs_ref.shape)
    align_ref[...] = align[:half]


def mine_kernel(align_ref, t1_ref, near_ref, mine_ref):
    mine_ref[...] = (near_ref[...] + profile_of(align_ref[...], t1_ref)).reshape(mine_ref.shape)


def final_kernel(scale, own_ref, message_ref, sims_ref, profile_ref, similarity_ref):
    count, rows = profile_ref.shape[:2]
    columns = similarity_ref.shape[1]
    total = (own_ref[...] + message_ref[0 : count * rows, :]) * scale
    for q in range(count):
        profile_ref[q] = total[q * rows : (q + 1) * rows]
    similarity_ref[...] = sims_ref[0:count, 0:columns] + message_ref[count * rows : count * rows + count, 0:columns]


def pack_kernel(mine_ref, theirs_ref, packed_ref, total_ref):
    total_ref[...] = mine_ref[...] + theirs_ref[...]
    top = jnp.max(jnp.abs(total_ref[...]), axis=0)
    top = jnp.max(jnp.max(top, axis=0, keepdims=True), axis=1, keepdims=True)
    power = jnp.floor(14.5 - jnp.log(jnp.maximum(top, 1e-30)) * (1.0 / math.log(2.0)))
    width = mine_ref.shape[2]
    packed_ref[:, :, :width] = total_ref[...] * jnp.exp2(power)[None]
    side = (mine_ref.shape[0], mine_ref.shape[1], packed_ref.shape[2] - width)
    packed_ref[:, :, width:] = jnp.broadcast_to(power[None], side)


def unpacked_sum(packed_ref, width):
    total = jnp.zeros((packed_ref.shape[1], width), F32)
    for n in range(packed_ref.shape[0]):
        total += packed_ref[n, :, :width] * jnp.exp2(-packed_ref[n, :, width : width + 1])
    return total


def hand_on(total, sims_ref, own_ref, message_ref):
    half = own_ref.shape[0]
    own_ref[...] = total[:half]
    message_ref[...] = jnp.zeros(message_ref.shape, F32)
    message_ref[0:half, :] = total[half:]
    message_ref[half : half + 2, 0 : sims_ref.shape[1]] = sims_ref[0:2, :]


def sum_kernel(packed_ref, total_ref):
    total_ref[...] = unpacked_sum(packed_ref, total_ref.shape[1])


def tail_kernel(pieces_ref, sims_ref, own_ref, message_ref):
    hand_on(jnp.sum(pieces_ref[...], axis=0), sims_ref, own_ref, message_ref)


def packed_tail_kernel(packed_ref, sims_ref, own_ref, message_ref):
    hand_on(unpacked_sum(packed_ref, own_ref.shape[1]), sims_ref, own_ref, message_ref)


SMEM = pl.BlockSpec(memory_space=pltpu.SMEM)
VMEM = pl.BlockSpec(memory_space=pltpu.VMEM)


def call(kernel, scalars, arrays, outs, flops, name, scratch=()):
    moved = sum(a.size * a.dtype.itemsize for a in [*arrays, *outs])
    return pl.pallas_call(
        kernel,
        out_shape=outs,
        in_specs=[SMEM] * len(scalars) + [VMEM] * len(arrays),
        out_specs=[VMEM] * len(outs),
        scratch_shapes=list(scratch),
        cost_estimate=pl.CostEstimate(flops=flops, bytes_accessed=moved, transcendentals=0),
        compiler_params=pltpu.CompilerParams(vmem_limit_bytes=20 << 20),
        name=name,
    )(*scalars, *arrays)


def moved_by(array, by):
    length = lax.axis_size(BLK)
    return lax.ppermute(array, BLK, [(i, (i + by) % length) for i in range(length)])


def shards(queries, query_lengths, targets, target_lengths):
    count, length, width = queries.shape
    blocks = targets.shape[0]
    profile_scale = 1.0 / math.sqrt(lax.axis_size(GRP) * blocks * (STEPS + 1))
    core = lax.axis_index("core").reshape(1)
    struct = jax.ShapeDtypeStruct
    pair_flops = 2 * count * blocks * length * length * width

    targets1 = moved_by(targets, 1)
    (mine2,) = call(
        fetch_kernel, [core, query_lengths], [queries], [struct((1, length, width), BF16)], queries.size, "fetch"
    )
    mine2 = moved_by(mine2, -2)
    lengths1 = moved_by(target_lengths, 1)

    sims_shape = struct((8, 128), F32)
    rows = count * length
    align, sims01 = call(
        own_kernel, [query_lengths, target_lengths], [queries, targets],
        [struct((rows, blocks * length), BF16), sims_shape], pair_flops, "own_pairs",
    )
    mine2, align = lax.optimization_barrier((mine2, align))
    other2 = lax.ppermute(mine2, "core", [(0, 1), (1, 0)])
    queries2 = jnp.where(core[0] == 0, jnp.concatenate([mine2, other2]), jnp.concatenate([other2, mine2]))
    partial_shape = struct((rows, width), F32)
    near_mine, near_theirs, sims23 = call(
        near_kernel, [core, target_lengths], [queries2, targets, align],
        [partial_shape, partial_shape, sims_shape], 3 * pair_flops, "near_pairs",
    )
    owned = rows // (NX * NZ)
    halves = struct((NX * NZ, owned, width), F32)
    theirs, align, sims01, sims23 = call(
        far_kernel, [core, query_lengths, lengths1], [queries, queries2, targets1, near_theirs, sims01, sims23],
        [halves, struct((rows, blocks * length), BF16), sims_shape, sims_shape], 3 * pair_flops, "far_pairs",
    )

    theirs = lax.ppermute(theirs, "core", [(0, 1), (1, 0)])
    (mine,) = call(mine_kernel, [], [align, targets1, near_mine], [halves], pair_flops, "own_rows")
    packed_shape = struct((NX * NZ, owned, width + 128), F32)
    (packed,) = call(
        pack_kernel, [], [mine, theirs], [packed_shape], 8 * mine.size, "pack", [pltpu.VMEM(mine.shape, F32)]
    )
    half = owned // 2
    ends = [struct((half, width), F32), struct((owned, width), F32)]
    packed = lax.all_to_all(packed.astype(jnp.float16), ("x", "zh"), 0, 0, tiled=True).astype(F32)
    own, message = call(packed_tail_kernel, [], [packed, sims23], ends, packed.size, "tail")
    message = moved_by(message, 2)
    profile, similarity = call(
        functools.partial(final_kernel, profile_scale), [], [own, message, sims01],
        [struct((count, half // count, width), F32), struct((count, blocks * (STEPS + 1)), F32)], own.size, "final",
    )
    return (profile, similarity)


def solution(mesh):
    cut = Mesh(mesh.devices.reshape(2, 8, NX, NZ, 2), BLK + GRP)
    in_specs = (P(BLK, None, None), P(BLK), P(BLK + GRP, None, None), P(BLK + GRP))
    out_specs = (P(BLK, GRP, None), P(BLK, GRP))
    return jax.shard_map(shards, mesh=cut, in_specs=in_specs, out_specs=out_specs, check_vma=False)
```
